32 devices in a mesh: groups: 2 (over x), tensor: 16 (over z, y, core).
Axes of the slice: x: 2, y: 2, z: 4, core: 2. Of those that a mesh axis runs over, the one named last changes fastest.
Arguments:
- tokens: bfloat16 [64, 8192], P(('groups', 'tensor')), parts along dimension 0, may hold values from -6 to 6
- gate_weight: bfloat16 [8192, 28672], P(None, 'tensor'), may hold values from -0.0625 to 0.0625
- up_weight: bfloat16 [8192, 28672], P(None, 'tensor'), may hold values from -0.0625 to 0.0625
- down_weight: bfloat16 [28672, 8192], P('tensor'), may hold values from -0.03125 to 0.03125
Outputs:
- mixed: bfloat16 [64, 8192], P(('groups', 'tensor')), parts along dimension 0
The draws below stay inside these ranges and needn't reach their ends.
There are 2 independent parts, one for each index of `groups`. The reference program is written for one: setup_inputs(seed, part) draws one part's arguments, and reference() takes and returns one part's arrays. A program takes and returns all parts, laid end to end along the dimension named above; an argument that names none is the same for every part. Nothing has to cross between parts.
All inputs are finite; a program needn't handle non-finite values.
Results may differ from the reference program's by a relative error of at most 0.015.
Values may be sent and summed in bfloat16 or wider, within the bound.
A program may use at most 128 MiB of HBM per device.

```python
import jax
import jax.numpy as jnp
import numpy as np
from jax import lax

D = 8192
FF = 28672
BLOCK = 32
TOKENS = 32
N_TENSOR = 16


def level_of(own_key, shape, pieces, low, top_value):
    def one(position, shards_of):
        heights = jax.random.uniform(jax.random.fold_in(jax.random.fold_in(own_key, 6), position), (shards_of,), jnp.float32, low / len(pieces), top_value / len(pieces))
        return jnp.repeat(jnp.exp(heights), shape[position] // shards_of).reshape((-1,) + (1,) * (len(shape) - position - 1))

    factor_of = one(*pieces[0])
    for cut in pieces[1:]:
        factor_of = factor_of * one(*cut)
    return factor_of


def normal_values(key, dims, spread, reach, pieces=(), kind=jnp.bfloat16):
    result = spread * jax.random.normal(key, dims, jnp.float32)
    if pieces:
        result = result * level_of(key, dims, pieces, -0.22, 0.18)
    return jnp.clip(result, -reach, reach).astype(kind)


def setup_inputs(seed: int = 0, part: int = 0) -> dict:
    keys = jax.random.split(jax.random.key(seed), 5)
    part_keys = jax.random.split(jax.random.fold_in(keys[4], part), 5)
    return {
        "tokens": normal_values(part_keys[0], (TOKENS, D), 1.0, 6.0, ((0, 16),)),
        "gate_weight": normal_values(keys[1], (D, FF), D ** -0.5, 0.0625, ((1, 16),)),
        "up_weight": normal_values(keys[2], (D, FF), D ** -0.5, 0.0625, ((1, 16),)),
        "down_weight": normal_values(keys[3], (FF, D), FF ** -0.5, 0.03125, ((0, 16),)),
    }


def walsh(order):
    index = np.arange(order)
    common = index[:, None] & index[None, :]
    parity = common * 0
    for shift in range(max(order.bit_length(), 1)):
        parity = parity ^ common >> shift & 1
    return (1 - 2 * parity).astype(np.float32)

def reference(tokens, gate_weight, up_weight, down_weight):
    gate = jnp.dot(tokens, gate_weight, preferred_element_type=jnp.float32)
    up = jnp.dot(tokens, up_weight, preferred_element_type=jnp.float32)
    hidden = jax.nn.silu(gate) * up
    width = FF // N_TENSOR
    shaped = hidden.reshape(TOKENS, N_TENSOR, width // BLOCK, BLOCK)
    outer = jnp.asarray(walsh(N_TENSOR), jnp.float32)
    inner = jnp.asarray(walsh(BLOCK), jnp.float32)
    turned = jnp.einsum('pq,tqbr,rs->tpbs', outer, shaped, inner, precision=lax.Precision.HIGHEST)
    turned = turned * (1.0 / np.sqrt(N_TENSOR * BLOCK))
    rotated = turned.reshape(TOKENS, FF).astype(jnp.bfloat16)
    return jnp.dot(rotated, down_weight, preferred_element_type=jnp.float32).astype(jnp.bfloat16)
```

```python
import functools

import jax
import jax.numpy as jnp
import numpy as np
from jax import lax
from jax.experimental import pallas as pl
from jax.experimental.pallas import tpu as pltpu
from jax.sharding import PartitionSpec as P

BLOCK = 32
COLS = 256
PAIRS = 4
SPLIT = 4
DOWNS = 6
CHUNKS = 4
LAG = 2
MESH = pl.DeviceIdType.MESH


def swapped(value, axis, stride):
    mask = 2**stride
    pairs = [(source, source ^ mask) for source in range(lax.axis_size(axis))]
    return lax.ppermute(value, axis, pairs)


def walsh(order):
    index = np.arange(order)
    common = index[:, None] & index[None, :]
    parity = common * 0
    for shift in range(max(order.bit_length(), 1)):
        parity = parity ^ common >> shift & 1
    return (1 - 2 * parity).astype(np.float32)


def plain(tokens, gate_weight, up_weight, down_weight):
    devices = lax.axis_size("tensor")
    width = gate_weight.shape[1]
    scale = 1.0 / np.sqrt(devices * BLOCK)
    inner = jnp.asarray(walsh(BLOCK), jnp.float32)
    piece = lax.all_gather(tokens, "tensor", axis=0, tiled=True)
    gate = jnp.dot(piece, gate_weight, preferred_element_type=jnp.float32)
    up = jnp.dot(piece, up_weight, preferred_element_type=jnp.float32)
    hidden = jax.nn.silu(gate) * up
    total = hidden.shape[0]
    local = jnp.einsum(
        "tbr,rs->tbs",
        hidden.reshape(total, width // BLOCK, BLOCK),
        inner,
        precision=lax.Precision.HIGHEST,
    ).reshape(total, width)
    index = lax.axis_index("tensor")
    for level in range(devices.bit_length() - 1):
        partner = swapped(local.astype(jnp.bfloat16), "tensor", level).astype(local.dtype)
        upper = index // (1 << level) % 2
        local = jnp.where(upper == 1, partner - local, local + partner)
    rotated = (local * scale).astype(jnp.bfloat16)
    terms = jnp.dot(rotated, down_weight, preferred_element_type=jnp.float32)
    mixed = lax.psum_scatter(terms, "tensor", scatter_dimension=0, tiled=True)
    return mixed.astype(jnp.bfloat16)


def parity(value, bits):
    total = value & 1
    for shift in range(1, bits):
        total = total ^ ((value >> shift) & 1)
    return total


def kernel(
    n,
    tokens,
    gate,
    up,
    down,
    out,
    gathered,
    lhs,
    acc,
    weights,
    downs,
    signs,
    rows,
    first_out,
    first_in,
    second_out,
    second_in,
    half_out,
    half_in,
    quarter_out,
    quarter_in,
    piece_out,
    piece_in,
    weight_sem,
    down_sem,
    gather_send,
    gather_recv,
    turn_send,
    turn_recv,
    sum_send,
    sum_recv,
):
    f32, bf16 = jnp.float32, jnp.bfloat16
    me = lax.axis_index("tensor")
    own, depth = tokens.shape
    total = n * own
    width = gate.shape[1]
    blocks = width // COLS
    outs = down.shape[1]
    bits = n.bit_length() - 1
    ring = n // 4
    scale = float(1.0 / np.sqrt(n * BLOCK))
    offset = [(i % ring) * 4 + (i // ring % 2) * 2 + i // (2 * ring) for i in range(n)]
    part = depth // SPLIT

    def weight_copy(which, b, piece):
        slot = lax.rem(b, PAIRS)
        source = (gate, up)[which]
        return pltpu.make_async_copy(
            source.at[pl.ds(piece * part, part), pl.ds(pl.multiple_of(b * COLS, COLS), COLS)],
            weights.at[slot, which, pl.ds(piece * part, part)],
            weight_sem.at[slot, which, piece],
        )

    def down_copy(b):
        slot = lax.rem(b, DOWNS)
        return pltpu.make_async_copy(
            down.at[pl.ds(pl.multiple_of(b * COLS, COLS), COLS)], downs.at[slot], down_sem.at[slot]
        )

    def start_weights(b):
        for piece in range(SPLIT):
            for which in range(2):
                weight_copy(which, b, piece).start()

    for b in range(min(PAIRS, blocks)):
        start_weights(jnp.int32(b))

    barrier = pltpu.get_barrier_semaphore()
    for i in range(1, n):
        pl.semaphore_signal(barrier, inc=1, device_id={"tensor": me ^ offset[i]}, device_id_type=MESH)
    pl.semaphore_wait(barrier, n - 1)

    def pass_on(source, slot, mask):
        return pltpu.make_async_remote_copy(
            src_ref=source,
            dst_ref=gathered.at[slot],
            send_sem=gather_send.at[slot],
            recv_sem=gather_recv.at[slot],
            device_id={"tensor": me ^ mask},
            device_id_type=MESH,
        )

    sends = []

    def send(source, slot, mask):
        copy = pass_on(source, slot, mask)
        copy.start()
        sends.append(copy)

    for i in range(1, ring):
        send(tokens, i, offset[i])
    send(tokens, ring, 2)
    send(tokens, 2 * ring, 1)

    one = lax.broadcasted_iota(jnp.int32, (COLS, COLS), 0)
    two = lax.broadcasted_iota(jnp.int32, (COLS, COLS), 1)
    sign = (1 - 2 * parity(one & two & (BLOCK - 1), BLOCK.bit_length() - 1)).astype(f32)
    signs[...] = jnp.where((one // BLOCK) == (two // BLOCK), sign, 0.0).astype(bf16)

    order = [ring]
    for i in range(1, ring):
        order.append(i)
        if i > 1:
            order.append(ring + i - 1)
    if ring > 1:
        order.append(2 * ring - 1)
    for i in order:
        pass_on(gathered.at[i], i, 1).wait_recv()
        if i < ring:
            send(gathered.at[i], ring + i, 2)
        send(gathered.at[i], 2 * ring + i, 1)
    for i in range(2 * ring, n):
        pass_on(gathered.at[i], i, 1).wait_recv()

    @pl.loop(0, depth // 1024)
    def _(c):
        columns = pl.ds(pl.multiple_of(c * 1024, 1024), 1024)
        for i in range(n):
            value = tokens[:, columns] if i == 0 else gathered[i, :, columns]
            acc[i * own : (i + 1) * own, columns] = value.astype(f32)
        lhs[:, columns] = acc[:, columns].astype(bf16)

    def exchange(source, target, which, b):
        return [
            pltpu.make_async_remote_copy(
                src_ref=source.at[b, i],
                dst_ref=target.at[b, i],
                send_sem=turn_send.at[which, b],
                recv_sem=turn_recv.at[which, b],
                device_id={"tensor": me ^ offset[i]},
                device_id_type=MESH,
            )
            for i in range(1, n)
        ]

    def all_of(source, target, which, b):
        return pltpu.make_async_remote_copy(
            src_ref=source.at[b, pl.ds(1, n - 1)],
            dst_ref=target.at[b, pl.ds(1, n - 1)],
            send_sem=turn_send.at[which, b],
            recv_sem=turn_recv.at[which, b],
            device_id={"tensor": me ^ 1},
            device_id_type=MESH,
        )

    flips = [(1 - 2 * parity(me & offset[i], bits)).astype(f32) for i in range(n)]
    whole = (1 - 2 * parity(me, bits)).astype(f32) * scale

    def across(b):
        all_of(first_out, first_in, 0, b).wait_recv()
        values = [first_in[b, i].astype(f32) * flips[i] for i in range(n)]
        step = 1
        while step < n:
            for i in range(n):
                if not i & step:
                    low, high = values[i], values[i + step]
                    values[i], values[i + step] = low + high, low - high
            step *= 2
        for i in range(n):
            target = second_in if i == 0 else second_out
            target[b, i] = (values[i] * (flips[i] * whole)).astype(bf16)
        for copy in exchange(second_out, second_in, 1, b):
            copy.start()

    @pl.loop(0, blocks)
    def _(b):
        slot = lax.rem(b, PAIRS)
        sums = [jnp.zeros((total, COLS), f32) for _ in range(2)]
        for piece in range(SPLIT):
            rows_of = pl.ds(piece * part, part)
            for which in range(2):
                weight_copy(which, b, piece).wait()
                sums[which] += jnp.dot(
                    lhs[:, rows_of], weights[slot, which, rows_of], preferred_element_type=f32
                )

        @pl.when(b + PAIRS < blocks)
        def _():
            start_weights(b + PAIRS)

        for e in range(pl.cdiv(DOWNS, PAIRS)):
            index = (b - max(blocks - PAIRS, 0)) * pl.cdiv(DOWNS, PAIRS) + e

            @pl.when((b + PAIRS >= blocks) & (index < min(DOWNS, blocks)))
            def _():
                down_copy(index).start()

        hidden = sums[0] / (1.0 + jnp.exp(-sums[0])) * sums[1]
        high = hidden.astype(bf16)
        low = (hidden - high.astype(f32)).astype(bf16)
        rows[...] = jnp.dot(high, signs[...], preferred_element_type=f32) + jnp.dot(
            low, signs[...], preferred_element_type=f32
        )
        for i in range(n):
            target = first_in if i == 0 else first_out
            target[b, i] = rows[i * own : (i + 1) * own, :].astype(bf16)
        for copy in exchange(first_out, first_in, 0, b):
            copy.start()

        @pl.when(b >= LAG)
        def _():
            across(b - LAG)

    def rotated(b):
        all_of(second_out, second_in, 1, b).wait_recv()
        for i in range(n):
            rows[i * own : (i + 1) * own, :] = second_in[b, i].astype(f32)
        down_copy(jnp.int32(b)).wait()
        return rows[...].astype(bf16)

    pending = list(range(max(blocks - LAG, 0), blocks))
    for b in range(blocks - 1):
        if pending and (b >= 1 or blocks - 1 - b <= len(pending)):
            if pending[0] != blocks - 1 or b >= 3 or b == blocks - 2:
                across(pending.pop(0))
        value = rotated(b)

        @pl.loop(0, outs // 1024)
        def _(c):
            columns = pl.ds(pl.multiple_of(c * 1024, 1024), 1024)
            term = jnp.dot(value, downs[b % DOWNS, :, columns], preferred_element_type=f32)
            if b:
                term = acc[:, columns] + term
            acc[:, columns] = term

        if b + DOWNS < blocks:
            down_copy(jnp.int32(b + DOWNS)).start()
    while pending:
        across(pending.pop(0))

    size = outs // CHUNKS
    half, quarter = total // 2, total // 4

    def sum_copy(level, c, source, target, mask, send_sem, recv_sem):
        return pltpu.make_async_remote_copy(
            src_ref=source,
            dst_ref=target,
            send_sem=send_sem,
            recv_sem=recv_sem,
            device_id={"tensor": me ^ mask},
            device_id_type=MESH,
        )

    def half_copy(c):
        return sum_copy(0, c, half_out.at[c], half_in.at[c], 1, sum_send.at[0, c], sum_recv.at[0, c])

    def quarter_copy(c):
        return sum_copy(
            1, c, quarter_out.at[c], quarter_in.at[c], 2, sum_send.at[1, c], sum_recv.at[1, c]
        )

    def piece_copy(c, i):
        return sum_copy(
            2,
            c,
            piece_out.at[c, i - 1],
            piece_in.at[c, i - 1],
            offset[i],
            sum_send.at[1 + i, c],
            sum_recv.at[1 + i, c],
        )

    last = rotated(blocks - 1)
    for c in range(CHUNKS):
        columns = pl.ds(c * size, size)
        term = jnp.dot(last, downs[(blocks - 1) % DOWNS, :, columns], preferred_element_type=f32)
        if blocks > 1:
            term = acc[:, columns] + term
        half_out[c] = term[half:].astype(bf16)
        acc[:half, columns] = term[:half]
        half_copy(c).start()
    for c in range(CHUNKS):
        columns = pl.ds(c * size, size)
        half_copy(c).wait_recv()
        term = acc[:half, columns] + half_in[c].astype(f32)
        quarter_out[c] = term[quarter:].astype(bf16)
        acc[:quarter, columns] = term[:quarter]
        quarter_copy(c).start()
    for c in range(CHUNKS):
        columns = pl.ds(c * size, size)
        quarter_copy(c).wait_recv()
        acc[:quarter, columns] = acc[:quarter, columns] + quarter_in[c].astype(f32)
        for i in range(1, ring):
            piece_out[c, i - 1] = acc[i * own : (i + 1) * own, columns].astype(bf16)
            piece_copy(c, i).start()
    for c in range(CHUNKS):
        columns = pl.ds(c * size, size)
        term = acc[:own, columns]
        for i in range(1, ring):
            piece_copy(c, i).wait_recv()
            term = term + piece_in[c, i - 1].astype(f32)
        out[:, columns] = term.astype(bf16)

    for copy in sends:
        copy.wait_send()
    for b in range(blocks):
        all_of(first_out, first_in, 0, b).wait_send()
        all_of(second_out, second_in, 1, b).wait_send()
    for c in range(CHUNKS):
        half_copy(c).wait_send()
        quarter_copy(c).wait_send()
        for i in range(1, ring):
            piece_copy(c, i).wait_send()


def fused(n, tokens, gate_weight, up_weight, down_weight):
    own, depth = tokens.shape
    total = n * own
    width = gate_weight.shape[1]
    blocks = width // COLS
    outs = down_weight.shape[1]
    ring = n // 4
    size = outs // CHUNKS
    bf16, f32 = jnp.bfloat16, jnp.float32
    turn = pltpu.VMEM((blocks, n, own, COLS), bf16)
    vmem = pl.BlockSpec(memory_space=pltpu.VMEM)
    anywhere = pl.BlockSpec(memory_space=pl.ANY)
    return pl.pallas_call(
        functools.partial(kernel, n),
        out_shape=jax.ShapeDtypeStruct((own, outs), bf16),
        in_specs=[vmem, anywhere, anywhere, anywhere],
        out_specs=vmem,
        scratch_shapes=[
            pltpu.VMEM((n, own, depth), bf16),
            pltpu.VMEM((total, depth), bf16),
            pltpu.VMEM((total, max(outs, depth)), f32),
            pltpu.VMEM((PAIRS, 2, depth, COLS), bf16),
            pltpu.VMEM((DOWNS, COLS, outs), bf16),
            pltpu.VMEM((COLS, COLS), bf16),
            pltpu.VMEM((total, COLS), f32),
            turn,
            turn,
            turn,
            turn,
            pltpu.VMEM((CHUNKS, total // 2, size), bf16),
            pltpu.VMEM((CHUNKS, total // 2, size), bf16),
            pltpu.VMEM((CHUNKS, total // 4, size), bf16),
            pltpu.VMEM((CHUNKS, total // 4, size), bf16),
            pltpu.VMEM((CHUNKS, ring - 1, own, size), bf16),
            pltpu.VMEM((CHUNKS, ring - 1, own, size), bf16),
            pltpu.SemaphoreType.DMA((PAIRS, 2, SPLIT)),
            pltpu.SemaphoreType.DMA((DOWNS,)),
            pltpu.SemaphoreType.DMA((n,)),
            pltpu.SemaphoreType.DMA((n,)),
            pltpu.SemaphoreType.DMA((2, blocks)),
            pltpu.SemaphoreType.DMA((2, blocks)),
            pltpu.SemaphoreType.DMA((1 + ring, CHUNKS)),
            pltpu.SemaphoreType.DMA((1 + ring, CHUNKS)),
        ],
        compiler_params=pltpu.CompilerParams(
            collective_id=0, has_side_effects=True, vmem_limit_bytes=67_000_000
        ),
    )(tokens, gate_weight, up_weight, down_weight)


def per_device(tokens, gate_weight, up_weight, down_weight):
    n = lax.axis_size("tensor")
    own, depth = tokens.shape
    width, outs = gate_weight.shape[1], down_weight.shape[1]
    held = 2 * COLS * (2 * PAIRS * depth + DOWNS * outs)
    fits = (
        8 <= n
        and n & (n - 1) == 0
        and width % COLS == 0
        and width // COLS > max(PAIRS, LAG)
        and n * own % 32 == 0
        and n * own <= 64
        and depth % (1024 * SPLIT) == 0
        and outs % (1024 * CHUNKS) == 0
        and held <= 60 << 20
    )
    if fits:
        return fused(n, tokens, gate_weight, up_weight, down_weight)
    return plain(tokens, gate_weight, up_weight, down_weight)


def solution(mesh):
    return jax.shard_map(
        per_device,
        mesh=mesh,
        in_specs=(
            P(("groups", "tensor"), None),
            P(None, "tensor"),
            P(None, "tensor"),
            P("tensor", None),
        ),
        out_specs=P(("groups", "tensor"), None),
        check_vma=False,
    )
```

```python
import functools

import jax
import jax.numpy as jnp
import numpy as np
from jax import lax
from jax.experimental import pallas as pl
from jax.experimental.pallas import tpu as pltpu
from jax.sharding import PartitionSpec as P

BLOCK = 32
COLS = 256
PAIRS = 4
SPLIT = 4
DOWNS = 6
CHUNKS = 4
GROUP = 3
LAG = 2
MESH = pl.DeviceIdType.MESH


def swapped(value, axis, stride):
    mask = 2**stride
    pairs = [(source, source ^ mask) for source in range(lax.axis_size(axis))]
    return lax.ppermute(value, axis, pairs)


def walsh(order):
    index = np.arange(order)
    common = index[:, None] & index[None, :]
    parity = common * 0
    for shift in range(max(order.bit_length(), 1)):
        parity = parity ^ common >> shift & 1
    return (1 - 2 * parity).astype(np.float32)


def plain(tokens, gate_weight, up_weight, down_weight):
    devices = lax.axis_size("tensor")
    width = gate_weight.shape[1]
    scale = 1.0 / np.sqrt(devices * BLOCK)
    inner = jnp.asarray(walsh(BLOCK), jnp.float32)
    piece = lax.all_gather(tokens, "tensor", axis=0, tiled=True)
    gate = jnp.dot(piece, gate_weight, preferred_element_type=jnp.float32)
    up = jnp.dot(piece, up_weight, preferred_element_type=jnp.float32)
    hidden = jax.nn.silu(gate) * up
    total = hidden.shape[0]
    local = jnp.einsum(
        "tbr,rs->tbs",
        hidden.reshape(total, width // BLOCK, BLOCK),
        inner,
        precision=lax.Precision.HIGHEST,
    ).reshape(total, width)
    index = lax.axis_index("tensor")
    for level in range(devices.bit_length() - 1):
        partner = swapped(local.astype(jnp.bfloat16), "tensor", level).astype(local.dtype)
        upper = index // (1 << level) % 2
        local = jnp.where(upper == 1, partner - local, local + partner)
    rotated = (local * scale).astype(jnp.bfloat16)
    terms = jnp.dot(rotated, down_weight, preferred_element_type=jnp.float32)
    mixed = lax.psum_scatter(terms, "tensor", scatter_dimension=0, tiled=True)
    return mixed.astype(jnp.bfloat16)


def parity(value, bits):
    total = value & 1
    for shift in range(1, bits):
        total = total ^ ((value >> shift) & 1)
    return total


def kernel(
    n,
    tokens,
    gate,
    up,
    down,
    out,
    gathered,
    lhs,
    acc,
    weights,
    downs,
    signs,
    rows,
    first_out,
    first_in,
    second_out,
    second_in,
    half_out,
    half_in,
    quarter_out,
    quarter_in,
    piece_out,
    piece_in,
    weight_sem,
    down_sem,
    gather_send,
    gather_recv,
    turn_send,
    turn_recv,
    sum_send,
    sum_recv,
):
    f32, bf16 = jnp.float32, jnp.bfloat16
    me = lax.axis_index("tensor")
    own, depth = tokens.shape
    total = n * own
    width = gate.shape[1]
    blocks = width // COLS
    outs = down.shape[1]
    bits = n.bit_length() - 1
    ring = n // 4
    scale = float(1.0 / np.sqrt(n * BLOCK))
    offset = [(i % ring) * 4 + (i // ring % 2) * 2 + i // (2 * ring) for i in range(n)]
    part = depth // SPLIT

    def weight_copy(which, b, piece):
        slot = lax.rem(b, PAIRS)
        source = (gate, up)[which]
        return pltpu.make_async_copy(
            source.at[pl.ds(piece * part, part), pl.ds(pl.multiple_of(b * COLS, COLS), COLS)],
            weights.at[slot, which, pl.ds(piece * part, part)],
            weight_sem.at[slot, which, piece],
        )

    def down_copy(b):
        slot = lax.rem(b, DOWNS)
        return pltpu.make_async_copy(
            down.at[pl.ds(pl.multiple_of(b * COLS, COLS), COLS)], downs.at[slot], down_sem.at[slot]
        )

    def start_weights(b):
        for piece in range(SPLIT):
            for which in range(2):
                weight_copy(which, b, piece).start()

    for b in range(min(PAIRS, blocks)):
        start_weights(jnp.int32(b))
    for b in range(min(DOWNS, blocks)):
        down_copy(jnp.int32(b)).start()

    barrier = pltpu.get_barrier_semaphore()
    for i in range(1, n):
        pl.semaphore_signal(barrier, inc=1, device_id={"tensor": me ^ offset[i]}, device_id_type=MESH)
    pl.semaphore_wait(barrier, n - 1)

    def pass_on(source, slot, mask):
        return pltpu.make_async_remote_copy(
            src_ref=source,
            dst_ref=gathered.at[slot],
            send_sem=gather_send.at[slot],
            recv_sem=gather_recv.at[slot],
            device_id={"tensor": me ^ mask},
            device_id_type=MESH,
        )

    sends = []

    def send(source, slot, mask):
        copy = pass_on(source, slot, mask)
        copy.start()
        sends.append(copy)

    for i in range(1, ring):
        send(tokens, i, offset[i])
    send(tokens, ring, 2)
    send(tokens, 2 * ring, 1)

    one = lax.broadcasted_iota(jnp.int32, (COLS, COLS), 0)
    two = lax.broadcasted_iota(jnp.int32, (COLS, COLS), 1)
    sign = (1 - 2 * parity(one & two & (BLOCK - 1), BLOCK.bit_length() - 1)).astype(f32)
    signs[...] = jnp.where((one // BLOCK) == (two // BLOCK), sign, 0.0).astype(bf16)

    order = [ring]
    for i in range(1, ring):
        order.append(i)
        if i > 1:
            order.append(ring + i - 1)
    if ring > 1:
        order.append(2 * ring - 1)
    for i in order:
        pass_on(gathered.at[i], i, 1).wait_recv()
        if i < ring:
            send(gathered.at[i], ring + i, 2)
        send(gathered.at[i], 2 * ring + i, 1)
    for i in range(2 * ring, n):
        pass_on(gathered.at[i], i, 1).wait_recv()

    @pl.loop(0, depth // 1024)
    def _(c):
        columns = pl.ds(pl.multiple_of(c * 1024, 1024), 1024)
        for i in range(n):
            value = tokens[:, columns] if i == 0 else gathered[i, :, columns]
            acc[i * own : (i + 1) * own, columns] = value.astype(f32)
        lhs[:, columns] = acc[:, columns].astype(bf16)

    groups = [(lo, min(lo + GROUP, blocks)) for lo in range(0, blocks, GROUP)]

    def exchange(source, target, which, g):
        lo, hi = groups[g]
        columns = pl.ds(lo * COLS, (hi - lo) * COLS)
        return [
            pltpu.make_async_remote_copy(
                src_ref=source.at[i, :, columns],
                dst_ref=target.at[i, :, columns],
                send_sem=turn_send.at[which, g],
                recv_sem=turn_recv.at[which, g],
                device_id={"tensor": me ^ offset[i]},
                device_id_type=MESH,
            )
            for i in range(1, n)
        ]

    def all_of(source, target, which, g):
        lo, hi = groups[g]
        part_of = (pl.ds(1, n - 1), slice(None), pl.ds(lo * COLS, (hi - lo) * COLS))
        return pltpu.make_async_remote_copy(
            src_ref=source.at[part_of],
            dst_ref=target.at[part_of],
            send_sem=turn_send.at[which, g],
            recv_sem=turn_recv.at[which, g],
            device_id={"tensor": me ^ 1},
            device_id_type=MESH,
        )

    flips = [(1 - 2 * parity(me & offset[i], bits)).astype(f32) for i in range(n)]
    whole = (1 - 2 * parity(me, bits)).astype(f32) * scale

    def across(g):
        all_of(first_out, first_in, 0, g).wait_recv()
        for b in range(*groups[g]):
            columns = pl.ds(b * COLS, COLS)
            values = [first_in[i, :, columns].astype(f32) * flips[i] for i in range(n)]
            step = 1
            while step < n:
                for i in range(n):
                    if not i & step:
                        low, high = values[i], values[i + step]
                        values[i], values[i + step] = low + high, low - high
                step *= 2
            for i in range(n):
                target = second_in if i == 0 else second_out
                target[i, :, columns] = (values[i] * (flips[i] * whole)).astype(bf16)
        for copy in exchange(second_out, second_in, 1, g):
            copy.start()

    def block(b):
        slot = lax.rem(b, PAIRS)
        sums = [jnp.zeros((total, COLS), f32) for _ in range(2)]
        for piece in range(SPLIT):
            rows_of = pl.ds(piece * part, part)
            for which in range(2):
                weight_copy(which, b, piece).wait()
                sums[which] += jnp.dot(
                    lhs[:, rows_of], weights[slot, which, rows_of], preferred_element_type=f32
                )

        @pl.when(b + PAIRS < blocks)
        def _():
            start_weights(b + PAIRS)

        hidden = sums[0] / (1.0 + jnp.exp(-sums[0])) * sums[1]
        high = hidden.astype(bf16)
        low = (hidden - high.astype(f32)).astype(bf16)
        rows[...] = jnp.dot(high, signs[...], preferred_element_type=f32) + jnp.dot(
            low, signs[...], preferred_element_type=f32
        )
        for i in range(n):
            target = first_in if i == 0 else first_out
            target[i, :, pl.ds(pl.multiple_of(b * COLS, COLS), COLS)] = rows[
                i * own : (i + 1) * own, :
            ].astype(bf16)

    begun = 0
    waiting = []
    for b in range(blocks):
        ends = [g for g, (_, hi) in enumerate(groups) if hi == b + 1]
        due = [g for g in waiting if groups[g][1] + LAG <= b + 1]
        if ends or due or b == blocks - 1:
            pl.loop(begun, b + 1)(block)
            begun = b + 1
        for g in ends:
            for copy in exchange(first_out, first_in, 0, g):
                copy.start()
            waiting.append(g)
        for g in due:
            across(g)
            waiting.remove(g)

    def rotated(b):
        g = b // GROUP
        if b == groups[g][0]:
            all_of(second_out, second_in, 1, g).wait_recv()
        columns = pl.ds(b * COLS, COLS)
        for i in range(n):
            rows[i * own : (i + 1) * own, :] = second_in[i, :, columns].astype(f32)
        down_copy(jnp.int32(b)).wait()
        return rows[...].astype(bf16)

    last_group = groups[-1][0]
    while len(waiting) > 1:
        across(waiting.pop(0))
    early = max(last_group - 1, blocks - DOWNS)
    for b in range(early):
        if waiting and b == min(2, early - 1):
            across(waiting.pop(0))
        value = rotated(b)

        @pl.loop(0, outs // 1024)
        def _(c):
            columns = pl.ds(pl.multiple_of(c * 1024, 1024), 1024)
            term = jnp.dot(value, downs[b % DOWNS, :, columns], preferred_element_type=f32)
            if b:
                term = acc[:, columns] + term
            acc[:, columns] = term

        if b + DOWNS < blocks:
            down_copy(jnp.int32(b + DOWNS)).start()
    while waiting:
        across(waiting.pop(0))

    size = outs // CHUNKS
    half, quarter = total // 2, total // 4

    def sum_copy(level, c, source, target, mask, send_sem, recv_sem):
        return pltpu.make_async_remote_copy(
            src_ref=source,
            dst_ref=target,
            send_sem=send_sem,
            recv_sem=recv_sem,
            device_id={"tensor": me ^ mask},
            device_id_type=MESH,
        )

    def half_copy(c):
        return sum_copy(0, c, half_out.at[c], half_in.at[c], 1, sum_send.at[0, c], sum_recv.at[0, c])

    def quarter_copy(c):
        return sum_copy(
            1, c, quarter_out.at[c], quarter_in.at[c], 2, sum_send.at[1, c], sum_recv.at[1, c]
        )

    def piece_copy(c, i):
        return sum_copy(
            2,
            c,
            piece_out.at[c, i - 1],
            piece_in.at[c, i - 1],
            offset[i],
            sum_send.at[1 + i, c],
            sum_recv.at[1 + i, c],
        )

    last = [(b, rotated(b)) for b in range(early, blocks)]
    for c in range(CHUNKS):
        columns = pl.ds(c * size, size)
        term = acc[:, columns]
        for b, value in last:
            term = term + jnp.dot(value, downs[b % DOWNS, :, columns], preferred_element_type=f32)
        half_out[c] = term[half:].astype(bf16)
        acc[:half, columns] = term[:half]
        half_copy(c).start()
    for c in range(CHUNKS):
        columns = pl.ds(c * size, size)
        half_copy(c).wait_recv()
        term = acc[:half, columns] + half_in[c].astype(f32)
        quarter_out[c] = term[quarter:].astype(bf16)
        acc[:quarter, columns] = term[:quarter]
        quarter_copy(c).start()
    for c in range(CHUNKS):
        columns = pl.ds(c * size, size)
        quarter_copy(c).wait_recv()
        acc[:quarter, columns] = acc[:quarter, columns] + quarter_in[c].astype(f32)
        for i in range(1, ring):
            piece_out[c, i - 1] = acc[i * own : (i + 1) * own, columns].astype(bf16)
            piece_copy(c, i).start()
    for c in range(CHUNKS):
        columns = pl.ds(c * size, size)
        term = acc[:own, columns]
        for i in range(1, ring):
            piece_copy(c, i).wait_recv()
            term = term + piece_in[c, i - 1].astype(f32)
        out[:, columns] = term.astype(bf16)

    for copy in sends:
        copy.wait_send()
    for g in range(len(groups)):
        all_of(first_out, first_in, 0, g).wait_send()
        all_of(second_out, second_in, 1, g).wait_send()
    for c in range(CHUNKS):
        half_copy(c).wait_send()
        quarter_copy(c).wait_send()
        for i in range(1, ring):
            piece_copy(c, i).wait_send()


def fused(n, tokens, gate_weight, up_weight, down_weight):
    own, depth = tokens.shape
    total = n * own
    width = gate_weight.shape[1]
    blocks = width // COLS
    outs = down_weight.shape[1]
    ring = n // 4
    size = outs // CHUNKS
    bf16, f32 = jnp.bfloat16, jnp.float32
    turn = pltpu.VMEM((n, own, width), bf16)
    vmem = pl.BlockSpec(memory_space=pltpu.VMEM)
    anywhere = pl.BlockSpec(memory_space=pl.ANY)
    return pl.pallas_call(
        functools.partial(kernel, n),
        out_shape=jax.ShapeDtypeStruct((own, outs), bf16),
        in_specs=[vmem, anywhere, anywhere, anywhere],
        out_specs=vmem,
        scratch_shapes=[
            pltpu.VMEM((n, own, depth), bf16),
            pltpu.VMEM((total, depth), bf16),
            pltpu.VMEM((total, max(outs, depth)), f32),
            pltpu.VMEM((PAIRS, 2, depth, COLS), bf16),
            pltpu.VMEM((DOWNS, COLS, outs), bf16),
            pltpu.VMEM((COLS, COLS), bf16),
            pltpu.VMEM((total, COLS), f32),
            turn,
            turn,
            turn,
            turn,
            pltpu.VMEM((CHUNKS, total // 2, size), bf16),
            pltpu.VMEM((CHUNKS, total // 2, size), bf16),
            pltpu.VMEM((CHUNKS, total // 4, size), bf16),
            pltpu.VMEM((CHUNKS, total // 4, size), bf16),
            pltpu.VMEM((CHUNKS, ring - 1, own, size), bf16),
            pltpu.VMEM((CHUNKS, ring - 1, own, size), bf16),
            pltpu.SemaphoreType.DMA((PAIRS, 2, SPLIT)),
            pltpu.SemaphoreType.DMA((DOWNS,)),
            pltpu.SemaphoreType.DMA((n,)),
            pltpu.SemaphoreType.DMA((n,)),
            pltpu.SemaphoreType.DMA((2, pl.cdiv(blocks, GROUP))),
            pltpu.SemaphoreType.DMA((2, pl.cdiv(blocks, GROUP))),
            pltpu.SemaphoreType.DMA((1 + ring, CHUNKS)),
            pltpu.SemaphoreType.DMA((1 + ring, CHUNKS)),
        ],
        compiler_params=pltpu.CompilerParams(
            collective_id=0, has_side_effects=True, vmem_limit_bytes=67_000_000
        ),
    )(tokens, gate_weight, up_weight, down_weight)


def per_device(tokens, gate_weight, up_weight, down_weight):
    n = lax.axis_size("tensor")
    own, depth = tokens.shape
    width, outs = gate_weight.shape[1], down_weight.shape[1]
    held = 2 * COLS * (2 * PAIRS * depth + DOWNS * outs)
    fits = (
        8 <= n
        and n & (n - 1) == 0
        and width % COLS == 0
        and width // COLS > max(PAIRS, LAG, GROUP, DOWNS)
        and n * own % 32 == 0
        and n * own <= 64
        and depth % (1024 * SPLIT) == 0
        and outs % (1024 * CHUNKS) == 0
        and held <= 60 << 20
    )
    if fits:
        return fused(n, tokens, gate_weight, up_weight, down_weight)
    return plain(tokens, gate_weight, up_weight, down_weight)


def solution(mesh):
    return jax.shard_map(
        per_device,
        mesh=mesh,
        in_specs=(
            P(("groups", "tensor"), None),
            P(None, "tensor"),
            P(None, "tensor"),
            P("tensor", None),
        ),
        out_specs=P(("groups", "tensor"), None),
        check_vma=False,
    )
```

```python
import functools

import jax
import jax.numpy as jnp
import numpy as np
from jax import lax
from jax.experimental import pallas as pl
from jax.experimental.pallas import tpu as pltpu
from jax.sharding import PartitionSpec as P

BLOCK = 32
COLS = 256
PAIRS = 4
SPLIT = 4
DOWNS = 6
CHUNKS = 4
GROUP = 3
LAG = 2
MESH = pl.DeviceIdType.MESH


def swapped(value, axis, stride):
    mask = 2**stride
    pairs = [(source, source ^ mask) for source in range(lax.axis_size(axis))]
    return lax.ppermute(value, axis, pairs)


def walsh(order):
    index = np.arange(order)
    common = index[:, None] & index[None, :]
    parity = common * 0
    for shift in range(max(order.bit_length(), 1)):
        parity = parity ^ common >> shift & 1
    return (1 - 2 * parity).astype(np.float32)


def plain(tokens, gate_weight, up_weight, down_weight):
    devices = lax.axis_size("tensor")
    width = gate_weight.shape[1]
    scale = 1.0 / np.sqrt(devices * BLOCK)
    inner = jnp.asarray(walsh(BLOCK), jnp.float32)
    piece = lax.all_gather(tokens, "tensor", axis=0, tiled=True)
    gate = jnp.dot(piece, gate_weight, preferred_element_type=jnp.float32)
    up = jnp.dot(piece, up_weight, preferred_element_type=jnp.float32)
    hidden = jax.nn.silu(gate) * up
    total = hidden.shape[0]
    local = jnp.einsum(
        "tbr,rs->tbs",
        hidden.reshape(total, width // BLOCK, BLOCK),
        inner,
        precision=lax.Precision.HIGHEST,
    ).reshape(total, width)
    index = lax.axis_index("tensor")
    for level in range(devices.bit_length() - 1):
        partner = swapped(local.astype(jnp.bfloat16), "tensor", level).astype(local.dtype)
        upper = index // (1 << level) % 2
        local = jnp.where(upper == 1, partner - local, local + partner)
    rotated = (local * scale).astype(jnp.bfloat16)
    terms = jnp.dot(rotated, down_weight, preferred_element_type=jnp.float32)
    mixed = lax.psum_scatter(terms, "tensor", scatter_dimension=0, tiled=True)
    return mixed.astype(jnp.bfloat16)


def parity(value, bits):
    total = value & 1
    for shift in range(1, bits):
        total = total ^ ((value >> shift) & 1)
    return total


def kernel(
    n,
    tokens,
    gate,
    up,
    down,
    out,
    gathered,
    lhs,
    acc,
    weights,
    downs,
    signs,
    rows,
    first_out,
    first_in,
    second_out,
    second_in,
    half_out,
    half_in,
    quarter_out,
    quarter_in,
    piece_out,
    piece_in,
    weight_sem,
    down_sem,
    gather_send,
    gather_recv,
    turn_send,
    turn_recv,
    sum_send,
    sum_recv,
):
    f32, bf16 = jnp.float32, jnp.bfloat16
    me = lax.axis_index("tensor")
    own, depth = tokens.shape
    total = n * own
    width = gate.shape[1]
    blocks = width // COLS
    outs = down.shape[1]
    bits = n.bit_length() - 1
    ring = n // 4
    scale = float(1.0 / np.sqrt(n * BLOCK))
    offset = [(i % ring) * 4 + (i // ring % 2) * 2 + i // (2 * ring) for i in range(n)]
    part = depth // SPLIT

    def weight_copy(which, b, piece):
        slot = lax.rem(b, PAIRS)
        source = (gate, up)[which]
        return pltpu.make_async_copy(
            source.at[pl.ds(piece * part, part), pl.ds(pl.multiple_of(b * COLS, COLS), COLS)],
            weights.at[slot, pl.ds(piece * part, part), pl.ds(which * COLS, COLS)],
            weight_sem.at[slot, which, piece],
        )

    def down_copy(b):
        slot = lax.rem(b, DOWNS)
        return pltpu.make_async_copy(
            down.at[pl.ds(pl.multiple_of(b * COLS, COLS), COLS)], downs.at[slot], down_sem.at[slot]
        )

    def start_weights(b):
        for piece in range(SPLIT):
            for which in range(2):
                weight_copy(which, b, piece).start()

    for b in range(min(PAIRS, blocks)):
        start_weights(jnp.int32(b))
    for b in range(min(DOWNS, blocks)):
        down_copy(jnp.int32(b)).start()

    barrier = pltpu.get_barrier_semaphore()
    for i in range(1, n):
        pl.semaphore_signal(barrier, inc=1, device_id={"tensor": me ^ offset[i]}, device_id_type=MESH)
    pl.semaphore_wait(barrier, n - 1)

    def pass_on(source, slot, mask):
        return pltpu.make_async_remote_copy(
            src_ref=source,
            dst_ref=gathered.at[slot],
            send_sem=gather_send.at[slot],
            recv_sem=gather_recv.at[slot],
            device_id={"tensor": me ^ mask},
            device_id_type=MESH,
        )

    sends = []

    def send(source, slot, mask):
        copy = pass_on(source, slot, mask)
        copy.start()
        sends.append(copy)

    for i in range(1, ring):
        send(tokens, i, offset[i])
    send(tokens, ring, 2)
    send(tokens, 2 * ring, 1)

    one = lax.broadcasted_iota(jnp.int32, (COLS, COLS), 0)
    two = lax.broadcasted_iota(jnp.int32, (COLS, COLS), 1)
    sign = (1 - 2 * parity(one & two & (BLOCK - 1), BLOCK.bit_length() - 1)).astype(f32)
    signs[...] = jnp.where((one // BLOCK) == (two // BLOCK), sign, 0.0).astype(bf16)

    order = [ring]
    for i in range(1, ring):
        order.append(i)
        if i > 1:
            order.append(ring + i - 1)
    if ring > 1:
        order.append(2 * ring - 1)
    for i in order:
        pass_on(gathered.at[i], i, 1).wait_recv()
        if i < ring:
            send(gathered.at[i], ring + i, 2)
        send(gathered.at[i], 2 * ring + i, 1)
    for i in range(2 * ring, n):
        pass_on(gathered.at[i], i, 1).wait_recv()

    @pl.loop(0, depth // 1024)
    def _(c):
        columns = pl.ds(pl.multiple_of(c * 1024, 1024), 1024)
        for i in range(n):
            value = tokens[:, columns] if i == 0 else gathered[i, :, columns]
            acc[i * own : (i + 1) * own, columns] = value.astype(f32)
        lhs[:, columns] = acc[:, columns].astype(bf16)

    groups = [(lo, min(lo + GROUP, blocks)) for lo in range(0, blocks, GROUP)]

    def exchange(source, target, which, g):
        lo, hi = groups[g]
        columns = pl.ds(lo * COLS, (hi - lo) * COLS)
        return [
            pltpu.make_async_remote_copy(
                src_ref=source.at[i, :, columns],
                dst_ref=target.at[i, :, columns],
                send_sem=turn_send.at[which, g],
                recv_sem=turn_recv.at[which, g],
                device_id={"tensor": me ^ offset[i]},
                device_id_type=MESH,
            )
            for i in range(1, n)
        ]

    def all_of(source, target, which, g):
        lo, hi = groups[g]
        part_of = (pl.ds(1, n - 1), slice(None), pl.ds(lo * COLS, (hi - lo) * COLS))
        return pltpu.make_async_remote_copy(
            src_ref=source.at[part_of],
            dst_ref=target.at[part_of],
            send_sem=turn_send.at[which, g],
            recv_sem=turn_recv.at[which, g],
            device_id={"tensor": me ^ 1},
            device_id_type=MESH,
        )

    flips = [(1 - 2 * parity(me & offset[i], bits)).astype(f32) for i in range(n)]
    whole = (1 - 2 * parity(me, bits)).astype(f32) * scale

    def across(g):
        all_of(first_out, first_in, 0, g).wait_recv()
        for b in range(*groups[g]):
            columns = pl.ds(b * COLS, COLS)
            values = [first_in[i, :, columns].astype(f32) * flips[i] for i in range(n)]
            step = 1
            while step < n:
                for i in range(n):
                    if not i & step:
                        low, high = values[i], values[i + step]
                        values[i], values[i + step] = low + high, low - high
                step *= 2
            for i in range(n):
                target = second_in if i == 0 else second_out
                target[i, :, columns] = (values[i] * (flips[i] * whole)).astype(bf16)
        for copy in exchange(second_out, second_in, 1, g):
            copy.start()

    def block(b):
        slot = lax.rem(b, PAIRS)
        sums = jnp.zeros((total, 2 * COLS), f32)
        for piece in range(SPLIT):
            rows_of = pl.ds(piece * part, part)
            for which in range(2):
                weight_copy(which, b, piece).wait()
            sums += jnp.dot(lhs[:, rows_of], weights[slot, rows_of, :], preferred_element_type=f32)

        @pl.when(b + PAIRS < blocks)
        def _():
            start_weights(b + PAIRS)

        left, right = sums[:, :COLS], sums[:, COLS:]
        hidden = left / (1.0 + jnp.exp(-left)) * right
        high = hidden.astype(bf16)
        low = (hidden - high.astype(f32)).astype(bf16)
        rows[...] = jnp.dot(high, signs[...], preferred_element_type=f32) + jnp.dot(
            low, signs[...], preferred_element_type=f32
        )
        for i in range(n):
            target = first_in if i == 0 else first_out
            target[i, :, pl.ds(pl.multiple_of(b * COLS, COLS), COLS)] = rows[
                i * own : (i + 1) * own, :
            ].astype(bf16)

    begun = 0
    waiting = []
    for b in range(blocks):
        ends = [g for g, (_, hi) in enumerate(groups) if hi == b + 1]
        due = [g for g in waiting if groups[g][1] + LAG <= b + 1]
        if ends or due or b == blocks - 1:
            pl.loop(begun, b + 1)(block)
            begun = b + 1
        for g in ends:
            for copy in exchange(first_out, first_in, 0, g):
                copy.start()
            waiting.append(g)
        for g in due:
            across(g)
            waiting.remove(g)

    def rotated(b):
        g = b // GROUP
        if b == groups[g][0]:
            all_of(second_out, second_in, 1, g).wait_recv()
        columns = pl.ds(b * COLS, COLS)
        for i in range(n):
            rows[i * own : (i + 1) * own, :] = second_in[i, :, columns].astype(f32)
        down_copy(jnp.int32(b)).wait()
        return rows[...].astype(bf16)

    last_group = groups[-1][0]
    while len(waiting) > 1:
        across(waiting.pop(0))
    early = max(last_group - 1, blocks - DOWNS)
    for b in range(early):
        if waiting and b == min(2, early - 1):
            across(waiting.pop(0))
        value = rotated(b)

        @pl.loop(0, outs // 1024)
        def _(c):
            columns = pl.ds(pl.multiple_of(c * 1024, 1024), 1024)
            term = jnp.dot(value, downs[b % DOWNS, :, columns], preferred_element_type=f32)
            if b:
                term = acc[:, columns] + term
            acc[:, columns] = term

        if b + DOWNS < blocks:
            down_copy(jnp.int32(b + DOWNS)).start()
    while waiting:
        across(waiting.pop(0))

    size = outs // CHUNKS
    half, quarter = total // 2, total // 4

    def sum_copy(level, c, source, target, mask, send_sem, recv_sem):
        return pltpu.make_async_remote_copy(
            src_ref=source,
            dst_ref=target,
            send_sem=send_sem,
            recv_sem=recv_sem,
            device_id={"tensor": me ^ mask},
            device_id_type=MESH,
        )

    def half_copy(c):
        return sum_copy(0, c, half_out.at[c], half_in.at[c], 1, sum_send.at[0, c], sum_recv.at[0, c])

    def quarter_copy(c):
        return sum_copy(
            1, c, quarter_out.at[c], quarter_in.at[c], 2, sum_send.at[1, c], sum_recv.at[1, c]
        )

    def piece_copy(c, i):
        return sum_copy(
            2,
            c,
            piece_out.at[c, i - 1],
            piece_in.at[c, i - 1],
            offset[i],
            sum_send.at[1 + i, c],
            sum_recv.at[1 + i, c],
        )

    last = [(b, rotated(b)) for b in range(early, blocks)]
    for c in range(CHUNKS):
        columns = pl.ds(c * size, size)
        term = acc[:, columns]
        for b, value in last:
            term = term + jnp.dot(value, downs[b % DOWNS, :, columns], preferred_element_type=f32)
        half_out[c] = term[half:].astype(bf16)
        acc[:half, columns] = term[:half]
        half_copy(c).start()
    for c in range(CHUNKS):
        columns = pl.ds(c * size, size)
        half_copy(c).wait_recv()
        term = acc[:half, columns] + half_in[c].astype(f32)
        quarter_out[c] = term[quarter:].astype(bf16)
        acc[:quarter, columns] = term[:quarter]
        quarter_copy(c).start()
    for c in range(CHUNKS):
        columns = pl.ds(c * size, size)
        quarter_copy(c).wait_recv()
        acc[:quarter, columns] = acc[:quarter, columns] + quarter_in[c].astype(f32)
        for i in range(1, ring):
            piece_out[c, i - 1] = acc[i * own : (i + 1) * own, columns].astype(bf16)
            piece_copy(c, i).start()
    for c in range(CHUNKS):
        columns = pl.ds(c * size, size)
        term = acc[:own, columns]
        for i in range(1, ring):
            piece_copy(c, i).wait_recv()
            term = term + piece_in[c, i - 1].astype(f32)
        out[:, columns] = term.astype(bf16)

    for copy in sends:
        copy.wait_send()
    for g in range(len(groups)):
        all_of(first_out, first_in, 0, g).wait_send()
        all_of(second_out, second_in, 1, g).wait_send()
    for c in range(CHUNKS):
        half_copy(c).wait_send()
        quarter_copy(c).wait_send()
        for i in range(1, ring):
            piece_copy(c, i).wait_send()


def fused(n, tokens, gate_weight, up_weight, down_weight):
    own, depth = tokens.shape
    total = n * own
    width = gate_weight.shape[1]
    blocks = width // COLS
    outs = down_weight.shape[1]
    ring = n // 4
    size = outs // CHUNKS
    bf16, f32 = jnp.bfloat16, jnp.float32
    turn = pltpu.VMEM((n, own, width), bf16)
    vmem = pl.BlockSpec(memory_space=pltpu.VMEM)
    anywhere = pl.BlockSpec(memory_space=pl.ANY)
    return pl.pallas_call(
        functools.partial(kernel, n),
        out_shape=jax.ShapeDtypeStruct((own, outs), bf16),
        in_specs=[vmem, anywhere, anywhere, anywhere],
        out_specs=vmem,
        scratch_shapes=[
            pltpu.VMEM((n, own, depth), bf16),
            pltpu.VMEM((total, depth), bf16),
            pltpu.VMEM((total, max(outs, depth)), f32),
            pltpu.VMEM((PAIRS, depth, 2 * COLS), bf16),
            pltpu.VMEM((DOWNS, COLS, outs), bf16),
            pltpu.VMEM((COLS, COLS), bf16),
            pltpu.VMEM((total, COLS), f32),
            turn,
            turn,
            turn,
            turn,
            pltpu.VMEM((CHUNKS, total // 2, size), bf16),
            pltpu.VMEM((CHUNKS, total // 2, size), bf16),
            pltpu.VMEM((CHUNKS, total // 4, size), bf16),
            pltpu.VMEM((CHUNKS, total // 4, size), bf16),
            pltpu.VMEM((CHUNKS, ring - 1, own, size), bf16),
            pltpu.VMEM((CHUNKS, ring - 1, own, size), bf16),
            pltpu.SemaphoreType.DMA((PAIRS, 2, SPLIT)),
            pltpu.SemaphoreType.DMA((DOWNS,)),
            pltpu.SemaphoreType.DMA((n,)),
            pltpu.SemaphoreType.DMA((n,)),
            pltpu.SemaphoreType.DMA((2, pl.cdiv(blocks, GROUP))),
            pltpu.SemaphoreType.DMA((2, pl.cdiv(blocks, GROUP))),
            pltpu.SemaphoreType.DMA((1 + ring, CHUNKS)),
            pltpu.SemaphoreType.DMA((1 + ring, CHUNKS)),
        ],
        compiler_params=pltpu.CompilerParams(
            collective_id=0, has_side_effects=True, vmem_limit_bytes=67_000_000
        ),
    )(tokens, gate_weight, up_weight, down_weight)


def per_device(tokens, gate_weight, up_weight, down_weight):
    n = lax.axis_size("tensor")
    own, depth = tokens.shape
    width, outs = gate_weight.shape[1], down_weight.shape[1]
    held = 2 * COLS * (2 * PAIRS * depth + DOWNS * outs)
    fits = (
        8 <= n
        and n & (n - 1) == 0
        and width % COLS == 0
        and width // COLS > max(PAIRS, LAG, GROUP, DOWNS)
        and n * own % 32 == 0
        and n * own <= 64
        and depth % (1024 * SPLIT) == 0
        and outs % (1024 * CHUNKS) == 0
        and held <= 60 << 20
    )
    if fits:
        return fused(n, tokens, gate_weight, up_weight, down_weight)
    return plain(tokens, gate_weight, up_weight, down_weight)


def solution(mesh):
    return jax.shard_map(
        per_device,
        mesh=mesh,
        in_specs=(
            P(("groups", "tensor"), None),
            P(None, "tensor"),
            P(None, "tensor"),
            P("tensor", None),
        ),
        out_specs=P(("groups", "tensor"), None),
        check_vma=False,
    )
```
